128 devices in a mesh: row: 8 (over z_hi, y), col: 8 (over x, core), dp: 2 (over z_lo).
Axes of the slice: x: 4, y: 4, z: 4 (z_hi: 2, z_lo: 2; z = z_hi * 2 + z_lo), core: 2. Of those that a mesh axis runs over, the one named last changes fastest.
Arguments:
- tokens: bfloat16 [2048, 8192], P(('dp', 'row'), 'col'), may hold values from -6 to 6
- w_in: bfloat16 [8192, 14336], P('col', 'row'), may hold values from -0.0625 to 0.0625
- w_out: bfloat16 [14336, 8192], P('row', 'col'), may hold values from -0.046875 to 0.046875
- spike_gain: float32 [14336], P('row'), may hold values from 1 to 4
- cotangent: bfloat16 [2048, 8192], P(('dp', 'row'), 'col'), may hold values from -1.5 to 1.5
Outputs:
- output: bfloat16 [2048, 8192], P(('dp', 'row'), 'col')
- grad_tokens: bfloat16 [2048, 8192], P(('dp', 'row'), 'col')
- grad_w_in: bfloat16 [8192, 14336], P('col', 'row')
- grad_w_out: bfloat16 [14336, 8192], P('row', 'col')
The draws below stay inside these ranges and needn't reach their ends.
All inputs are finite; a program needn't handle non-finite values.
Results may differ from the reference program's by a relative error of at most 0.035.
Values may be sent and summed in bfloat16 or wider, within the bound.
A program may use at most 128 MiB of HBM per device.

```python
import math
import jax
import jax.numpy as jnp
from jax import lax

D = 8192
FF = 14336
LEVELS = 4
TOKENS = 2048
N_ROW = 8
N_COL = 8
N_DP = 2


def steps_of(stream_key, dims, pieces, least, top_value):
    loudness, own = 1.0, jax.random.fold_in(stream_key, 6)
    for position, blocks in pieces:
        heights = jnp.exp(jax.random.uniform(jax.random.fold_in(own, position), (blocks,), jnp.float32, least / len(pieces), top_value / len(pieces)))
        loudness = loudness * jnp.repeat(heights, dims[position] // blocks).reshape([-1 if axis == position else 1 for axis in range(len(dims))])
    return loudness


def gaussian(rng, extent, spread, reach, cuts=(), held_as=jnp.bfloat16):
    drawn = jax.random.normal(rng, extent, jnp.float32) * spread
    if len(cuts) > 0:
        drawn = steps_of(rng, extent, cuts, -0.22, 0.18) * drawn
    return jnp.clip(drawn, min=-reach, max=reach).astype(held_as)


def setup_inputs(seed: int = 0) -> dict:
    splits = jax.random.split(jax.random.key(seed), 6)
    return {
        "tokens": gaussian(splits[0], (TOKENS, D), 1.0, 6.0, ((0, 16), (1, 8))),
        "w_in": gaussian(splits[1], (D, FF), D ** -0.5, 0.0625, ((0, 8), (1, 8))),
        "w_out": gaussian(splits[2], (FF, D), FF ** -0.5, 0.046875, ((0, 8), (1, 8))),
        "spike_gain": jnp.clip(jnp.exp(math.log(4.0) - 1.3862944 * jax.random.uniform(splits[3], (FF,), jnp.float32) ** steps_of(splits[3], (FF,), ((0, 8),), -0.2, 0.2)), 1.0, 4.0),
        "cotangent": gaussian(splits[4], (TOKENS, D), 0.25, 1.5, ((0, 16), (1, 8))),
    }


sharpness = 4.0


def rounded(value):
    return lax.optimization_barrier(value.astype(jnp.bfloat16)).astype(jnp.float32)


def spike_parts(potential, gain):
    scaled = potential * gain[None, :]
    total = jnp.zeros_like(scaled)
    slope = jnp.zeros_like(scaled)
    for level in range(LEVELS):
        sig = jax.nn.sigmoid(sharpness * (scaled - (level + 0.5)))
        total = total + sig
        slope = slope + sig * (1.0 - sig)
    return total, slope * (sharpness * gain[None, :])


def reference(tokens, w_in, w_out, spike_gain, cotangent):
    feat = D // N_COL
    hid = FF // N_ROW
    run = TOKENS // N_DP
    potential = jnp.zeros((TOKENS, FF), jnp.float32)
    for block in range(N_COL):
        part = jnp.dot(tokens[:, block * feat:(block + 1) * feat], w_in[block * feat:(block + 1) * feat, :], preferred_element_type=jnp.float32)
        potential = potential + rounded(part)
    total, slope = spike_parts(potential, spike_gain)
    spikes = total.astype(jnp.bfloat16)
    output = jnp.zeros((TOKENS, D), jnp.float32)
    for block in range(N_ROW):
        part = jnp.dot(spikes[:, block * hid:(block + 1) * hid], w_out[block * hid:(block + 1) * hid, :], preferred_element_type=jnp.float32)
        output = output + rounded(part)
    grad_spikes = jnp.zeros((TOKENS, FF), jnp.float32)
    for block in range(N_COL):
        part = jnp.dot(cotangent[:, block * feat:(block + 1) * feat], w_out[:, block * feat:(block + 1) * feat].T, preferred_element_type=jnp.float32)
        grad_spikes = grad_spikes + rounded(part)
    grad_potential = (grad_spikes * slope).astype(jnp.bfloat16)
    grad_tokens = jnp.zeros((TOKENS, D), jnp.float32)
    for block in range(N_ROW):
        part = jnp.dot(grad_potential[:, block * hid:(block + 1) * hid], w_in[:, block * hid:(block + 1) * hid].T, preferred_element_type=jnp.float32)
        grad_tokens = grad_tokens + rounded(part)
    grad_w_in = jnp.zeros((D, FF), jnp.float32)
    grad_w_out = jnp.zeros((FF, D), jnp.float32)
    for half in range(N_DP):
        lower = half * run
        upper = (half + 1) * run
        grad_w_in = grad_w_in + rounded(jnp.dot(tokens[lower:upper].T, grad_potential[lower:upper], preferred_element_type=jnp.float32))
        grad_w_out = grad_w_out + rounded(jnp.dot(spikes[lower:upper].T, cotangent[lower:upper], preferred_element_type=jnp.float32))
    return (output.astype(jnp.bfloat16), grad_tokens.astype(jnp.bfloat16), grad_w_in.astype(jnp.bfloat16), grad_w_out.astype(jnp.bfloat16))
```

```python
import jax
import jax.numpy as jnp
from jax import lax
from jax.experimental import pallas as pl
from jax.experimental.pallas import tpu as pltpu
from jax.sharding import PartitionSpec as P

LEVELS = 4
SHARP = 4.0
BF = jnp.bfloat16
F32 = jnp.float32
FEAT, HID, BLK = 1024, 1792, 128
SUB = 32
TILE = 256

NAMES = (
    ["za", "zb", "zc", "zd", "ze", "zf"]
    + ["ya", "yb", "yc", "yd", "ye", "yf", "yg", "yh", "oa", "ob", "oc", "od"]
    + [f"{n}{k}" for k in range(4) for n in (
        "r1", "r2p", "r2m", "r3p", "r3m",
        "gp", "gm", "gd", "g2p", "g2m", "g3",
        "hp", "hm", "h2p", "h2m", "h3")]
    + [f"{n}{k}" for k in range(2) for n in ("d2p", "d2m", "dep", "dem", "dlp", "dlm", "dz")]
)
INDEX = {name: i for i, name in enumerate(NAMES)}


def nn(a, b):
    return lax.dot_general(a, b, (((1,), (0,)), ((), ())), preferred_element_type=F32)


def nt(a, b):
    return lax.dot_general(a, b, (((1,), (1,)), ((), ())), preferred_element_type=F32)


def tn(a, b):
    return lax.dot_general(a, b, (((0,), (0,)), ((), ())), preferred_element_type=F32)


def kernel(tok_h, win_h, wout_h, gain_h, cot_h,
           out_h, gtok_h, gwin_h, gwout_h,
           win, wout, gain, TC, PP, RB, X2, X1, SG, OP, YB2, YB1, ZS, ZB, OS, WI, WO,
           ssem, rsem, lsem):
    row, col, d = lax.axis_index("row"), lax.axis_index("col"), lax.axis_index("dp")
    zh, y = row // 4, row % 4
    x, c = col // 2, col % 2
    z = 2 * zh + d
    sib = 1 - c

    def dev(xx=None, cc=None, yy=None, zz=None):
        xx = x if xx is None else xx
        cc = c if cc is None else cc
        yy = y if yy is None else yy
        zz = z if zz is None else zz
        return (4 * (zz // 2) + yy, 2 * xx + cc, zz % 2)

    xp, xm, xo = (x + 1) % 4, (x + 3) % 4, (x + 2) % 4
    yp, ym, yo = (y + 1) % 4, (y + 3) % 4, (y + 2) % 4
    zp, zm, zo = (z + 1) % 4, (z + 3) % 4, (z + 2) % 4
    to_xp, to_xm = dev(xx=xp), dev(xx=xm)
    to_yp, to_ym = dev(yy=yp), dev(yy=ym)
    to_zp, to_zm, to_zo = dev(zz=zp), dev(zz=zm), dev(zz=zo)
    to_sib = dev(cc=sib)
    to_dp = (row, col, 1 - d)

    sent = {}

    def send(name, src, dst, to):
        i = INDEX[name]
        copy = pltpu.make_async_remote_copy(
            src_ref=src, dst_ref=dst, send_sem=ssem.at[i], recv_sem=rsem.at[i],
            device_id=to, device_id_type=pl.DeviceIdType.MESH)
        copy.start()
        sent[name] = copy

    def got(*names):
        for name in names:
            sent[name].wait_recv()

    loads = [
        pltpu.make_async_copy(tok_h, TC.at[d, 0, y, zh], lsem.at[0]),
        pltpu.make_async_copy(cot_h, TC.at[d, 1, y, zh], lsem.at[1]),
        pltpu.make_async_copy(win_h, win, lsem.at[2]),
        pltpu.make_async_copy(wout_h, wout, lsem.at[3]),
        pltpu.make_async_copy(gain_h, gain, lsem.at[4]),
    ]
    for load in loads:
        load.start()
    barrier = pltpu.get_barrier_semaphore()
    for to in (to_xp, to_xm, to_yp, to_ym, to_zp, to_zm, to_zo, to_sib):
        pl.semaphore_signal(barrier, inc=1, device_id=to, device_id_type=pl.DeviceIdType.MESH)
    pl.semaphore_wait(barrier, 8)
    loads[0].wait()
    loads[1].wait()

    H0, H1 = pl.ds(0, 64), pl.ds(64, 64)

    def tc(dd, yy, hh, rows=None):
        return TC.at[dd, :, yy, hh] if rows is None else TC.at[dd, :, yy, hh, rows]

    def zslot(zz, rows):
        return tc(zz % 2, y, zz // 2, rows)

    def same(name, ref, to):
        send(name, ref, ref, to)

    same("za", zslot(z, H0), to_zp)
    same("zb", zslot(z, H1), to_zm)
    same("ya", tc(d, y, zh), to_yp)
    same("yb", tc(d, y, zh), to_ym)
    got("za")
    same("ze", zslot(zm, H0), to_zp)
    got("zb")
    same("zf", zslot(zp, H1), to_zm)
    same("zc", zslot(z, H1), to_zp)
    same("zd", zslot(z, H0), to_zm)
    for load in loads[2:]:
        load.wait()

    def chunk(k):
        return (y + k) % 4

    def first_products(k):
        yy = chunk(k)

        def tile(n, carry):
            cols = pl.ds(pl.multiple_of(n * TILE, TILE), TILE)
            a = TC[d, 0, yy].reshape(2 * BLK, FEAT)
            PP[k, 0, :, :, :, cols] = nn(a, win[:, cols]).astype(BF).reshape(2, 4, SUB, TILE)
            b = TC[d, 1, yy].reshape(2 * BLK, FEAT)
            PP[k, 1, :, :, :, cols] = nt(b, wout[cols, :]).astype(BF).reshape(2, 4, SUB, TILE)
            return carry

        lax.fori_loop(0, HID // TILE, tile, 0)
        send(f"r1{k}", PP.at[k, :, sib], RB.at[k], to_sib)

    def pair(k, kind, q):
        return PP[k, kind, c, q].astype(F32) + RB[k, kind, q].astype(F32)

    def reduce_far(k):
        got(f"r1{k}")
        for kind in range(2):
            PP[k, kind, c, xo] = pair(k, kind, xo).astype(BF)
        send(f"r2p{k}", PP.at[k, :, c, xo, pl.ds(0, 16)], X2.at[k, 0], to_xp)
        send(f"r2m{k}", PP.at[k, :, c, xo, pl.ds(16, 16)], X2.at[k, 1], to_xm)

    def reduce_near(k):
        for name, q, way, to in (("r2p", xp, 0, to_xp), ("r2m", xm, 1, to_xm)):
            got(f"{name}{k}")
            for kind in range(2):
                both = pair(k, kind, q).reshape(2, 16, HID)
                add = X2[k, way, kind].astype(F32)
                parts = [both[0], both[1]]
                parts[way] = parts[way] + add
                PP[k, kind, c, q] = jnp.stack(parts).reshape(SUB, HID).astype(BF)
            send(f"r3{'pm'[way]}{k}", PP.at[k, :, c, q], X1.at[k, way], to)

    def activate(k):
        got(f"r3p{k}", f"r3m{k}")
        yy = chunk(k)
        sums = [
            pair(k, kind, x) + X1[k, 0, kind].astype(F32) + X1[k, 1, kind].astype(F32)
            for kind in range(2)
        ]
        g = gain[...]
        scaled = sums[0] * g
        total = jnp.zeros_like(scaled)
        slope = jnp.zeros_like(scaled)
        for level in range(LEVELS):
            sig = jax.nn.sigmoid(SHARP * (scaled - (level + 0.5)))
            total = total + sig
            slope = slope + sig * (1.0 - sig)
        SG[d, 0, yy, c, x] = total.astype(BF)
        SG[d, 1, yy, c, x] = (sums[1] * (slope * (SHARP * g))).astype(BF)
        block = SG.at[d, :, yy, c, x]
        same(f"gp{k}", block, to_xp)
        same(f"gm{k}", block, to_xm)
        same(f"gd{k}", block, to_dp)

    def share_other(k):
        got(f"gd{k}")
        block = SG.at[1 - d, :, chunk(k), c, x]
        same(f"hp{k}", block, to_xp)
        same(f"hm{k}", block, to_xm)

    def forward(k, g, dd):
        yy = chunk(k)
        got(f"{g}p{k}")
        same(f"{g}2p{k}", SG.at[dd, :, yy, c, xm, pl.ds(0, 16)], to_xp)
        got(f"{g}m{k}")
        same(f"{g}2m{k}", SG.at[dd, :, yy, c, xp, pl.ds(16, 16)], to_xm)

    def to_sibling(k, g, dd):
        got(f"{g}2p{k}", f"{g}2m{k}")
        same(f"{g}3{k}", SG.at[dd, :, chunk(k), c], to_sib)

    def second_products(k):
        got(f"g3{k}")
        yy = chunk(k)

        def tile(n, carry):
            cols = pl.ds(pl.multiple_of(n * TILE, TILE), TILE)
            a = SG[d, 0, yy].reshape(2 * BLK, HID)
            OP[k, 0, :, :, cols] = nn(a, wout[:, cols]).astype(BF).reshape(2, BLK, TILE)
            b = SG[d, 1, yy].reshape(2 * BLK, HID)
            OP[k, 1, :, :, cols] = nt(b, win[cols, :]).astype(BF).reshape(2, BLK, TILE)
            return carry

        lax.fori_loop(0, FEAT // TILE, tile, 0)

    def out_far(kind):
        send(f"d2p{kind}", OP.at[2, kind, 0], YB2.at[0, kind], to_yp)
        send(f"d2m{kind}", OP.at[2, kind, 1], YB2.at[1, kind], to_ym)

    def out_early(kind):
        send(f"dep{kind}", OP.at[1, kind, 1], YB1.at[0, kind, 1], to_yp)
        send(f"dem{kind}", OP.at[3, kind, 0], YB1.at[1, kind, 0], to_ym)

    def strips(fn):
        def strip(i, carry):
            fn(pl.ds(pl.multiple_of(i * SUB, SUB), SUB))
            return carry
        lax.fori_loop(0, BLK // SUB, strip, 0)

    def out_late(kind):
        for name, k, half, way, to in (("d2p", 1, 0, 0, to_yp), ("d2m", 3, 1, 1, to_ym)):
            got(f"{name}{kind}")

            def add(rows):
                OP[k, kind, half, rows] = (
                    OP[k, kind, half, rows].astype(F32) + YB2[way, kind, rows].astype(F32)
                ).astype(BF)

            strips(add)
            send(f"dl{'pm'[way]}{kind}", OP.at[k, kind, half], YB1.at[way, kind, half], to)

    def out_sum(kind, half, rows):
        return (OP[0, kind, half, rows].astype(F32) + YB1[0, kind, half, rows].astype(F32)
                + YB1[1, kind, half, rows].astype(F32))

    def out_across(kind):
        got(f"dep{kind}", f"dem{kind}", f"dlp{kind}", f"dlm{kind}")

        def add(rows):
            ZS[kind, rows] = out_sum(kind, 1 - zh, rows).astype(BF)

        strips(add)
        send(f"dz{kind}", ZS.at[kind], ZB.at[kind], to_zo)

    stores = []

    def store(src, dst, i):
        copy = pltpu.make_async_copy(src, dst, lsem.at[i])
        copy.start()
        stores.append(copy)

    def out_final(kind):
        got(f"dz{kind}")

        def add(rows):
            OS[kind, rows] = (out_sum(kind, zh, rows) + ZB[kind, rows].astype(F32)).astype(BF)

        strips(add)
        store(OS.at[kind], (out_h, gtok_h)[kind], 5 + kind)

    def grad_in(dd, first):
        b = 4 * 2 * BLK

        def tile(n, carry):
            cols = pl.ds(pl.multiple_of(n * TILE, TILE), TILE)
            left = TC[dd, 0, :, :, :, cols].reshape(b, TILE)
            value = tn(left, SG[dd, 1].reshape(b, HID))
            if not first:
                value = value + WI[cols, :].astype(F32)
            WI[cols, :] = value.astype(BF)
            return carry

        lax.fori_loop(0, FEAT // TILE, tile, 0)

    def grad_out(dd, first):
        b = 4 * 2 * BLK

        def tile(n, carry):
            cols = pl.ds(pl.multiple_of(n * TILE, TILE), TILE)
            left = SG[dd, 0, :, :, :, :, cols].reshape(b, TILE)
            value = tn(left, TC[dd, 1].reshape(b, FEAT))
            if not first:
                value = value + WO[cols, :].astype(F32)
            WO[cols, :] = value.astype(BF)
            return carry

        lax.fori_loop(0, HID // TILE, tile, 0)

    got("ze", "zf")
    same("yc", tc(d, y, 1 - zh), to_yp)
    same("yd", tc(d, y, 1 - zh), to_ym)
    first_products(0)
    got("ya")
    same("ye", tc(d, ym, zh, H0), to_yp)
    got("yb")
    same("yf", tc(d, yp, zh, H1), to_ym)
    reduce_far(0)
    got("yc")
    same("yg", tc(d, ym, 1 - zh, H0), to_yp)
    got("yd")
    same("yh", tc(d, yp, 1 - zh, H1), to_ym)
    first_products(3)
    first_products(1)
    reduce_near(0)
    reduce_far(3)
    reduce_far(1)
    got("zc", "zd")
    activate(0)
    same("oa", TC.at[1 - d, :, y], to_yp)
    same("ob", TC.at[1 - d, :, y], to_ym)
    got("ye", "yf", "yg", "yh")
    first_products(2)
    reduce_near(3)
    reduce_near(1)
    reduce_far(2)
    forward(0, "g", d)
    activate(3)
    activate(1)
    reduce_near(2)
    to_sibling(0, "g", d)
    forward(3, "g", d)
    forward(1, "g", d)
    activate(2)
    second_products(0)
    to_sibling(3, "g", d)
    to_sibling(1, "g", d)
    forward(2, "g", d)
    got("oa")
    same("oc", TC.at[1 - d, :, ym, 0], to_yp)
    got("ob")
    same("od", TC.at[1 - d, :, yp, 1], to_ym)
    share_other(0)
    second_products(3)
    second_products(1)
    out_early(0)
    out_early(1)
    to_sibling(2, "g", d)
    share_other(3)
    share_other(1)
    forward(0, "h", 1 - d)
    second_products(2)
    out_far(0)
    out_far(1)
    share_other(2)
    to_sibling(0, "h", 1 - d)
    grad_out(d, True)
    forward(3, "h", 1 - d)
    forward(1, "h", 1 - d)
    out_late(0)
    out_late(1)
    to_sibling(3, "h", 1 - d)
    to_sibling(1, "h", 1 - d)
    forward(2, "h", 1 - d)
    grad_in(d, True)
    to_sibling(2, "h", 1 - d)
    out_across(0)
    out_across(1)
    got("oc", "od")
    got(*[f"h3{k}" for k in range(4)])
    grad_out(1 - d, False)
    store(WO, gwout_h, 7)
    out_final(0)
    out_final(1)
    grad_in(1 - d, False)
    store(WI, gwin_h, 8)
    for copy in stores:
        copy.wait()
    for name in NAMES:
        sent[name].wait_send()


def shards(tokens, w_in, w_out, spike_gain, cotangent):
    anywhere = pl.BlockSpec(memory_space=pl.ANY)
    vmem = pltpu.VMEM
    n = len(NAMES)
    return pl.pallas_call(
        kernel,
        out_shape=(
            jax.ShapeDtypeStruct((BLK, FEAT), BF),
            jax.ShapeDtypeStruct((BLK, FEAT), BF),
            jax.ShapeDtypeStruct((FEAT, HID), BF),
            jax.ShapeDtypeStruct((HID, FEAT), BF),
        ),
        in_specs=[anywhere] * 5,
        out_specs=[anywhere] * 4,
        scratch_shapes=[
            vmem((FEAT, HID), BF),
            vmem((HID, FEAT), BF),
            vmem((1, HID), F32),
            vmem((2, 2, 4, 2, BLK, FEAT), BF),
            vmem((4, 2, 2, 4, SUB, HID), BF),
            vmem((4, 2, 4, SUB, HID), BF),
            vmem((4, 2, 2, 16, HID), BF),
            vmem((4, 2, 2, SUB, HID), BF),
            vmem((2, 2, 4, 2, 4, SUB, HID), BF),
            vmem((4, 2, 2, BLK, FEAT), BF),
            vmem((2, 2, BLK, FEAT), BF),
            vmem((2, 2, 2, BLK, FEAT), BF),
            vmem((2, BLK, FEAT), BF),
            vmem((2, BLK, FEAT), BF),
            vmem((2, BLK, FEAT), BF),
            vmem((FEAT, HID), BF),
            vmem((HID, FEAT), BF),
            pltpu.SemaphoreType.DMA((n,)),
            pltpu.SemaphoreType.DMA((n,)),
            pltpu.SemaphoreType.DMA((9,)),
        ],
        compiler_params=pltpu.CompilerParams(
            collective_id=0, has_side_effects=True, vmem_limit_bytes=64 << 20
        ),
        name="spiking_block",
    )(tokens, w_in, w_out, spike_gain.reshape(1, HID), cotangent)


def solution(mesh):
    placed = (
        P(("dp", "row"), "col"),
        P("col", "row"),
        P("row", "col"),
        P("row"),
        P(("dp", "row"), "col"),
    )
    return jax.shard_map(
        shards,
        mesh=mesh,
        in_specs=placed,
        out_specs=(
            P(("dp", "row"), "col"),
            P(("dp", "row"), "col"),
            P("col", "row"),
            P("row", "col"),
        ),
        check_vma=False,
    )
```

```python
import jax
import jax.numpy as jnp
from jax import lax
from jax.experimental import pallas as pl
from jax.experimental.pallas import tpu as pltpu
from jax.sharding import PartitionSpec as P

LEVELS = 4
SHARP = 4.0
BF = jnp.bfloat16
F32 = jnp.float32
FEAT, HID, BLK = 1024, 1792, 128
SUB = 16
TILE = 256

DIRECT = (4, 0)

ORDER = [
    "I", "L", "A0", "B0", "Z2", "Z1", "C0", "D0", "A6", "Y3", "Y2", "A2", "Y1", "A1", "E0", "B6", "B2", "P6",
    "Z3", "P2", "B1", "F0", "A4", "M0", "C2", "C6", "B4", "P4", "C1", "D2", "D6", "C4", "A3", "Y5", "A7",
    "D1", "E2", "B3", "P3", "Y4", "P7", "B7", "E6", "D4", "E1", "F2", "C3", "A5", "P5", "M2", "C7", "J0",
    "B5", "F6", "E4", "M6", "F1", "D3", "D7", "M1", "C5", "F4", "M4", "E3", "E7", "D5", "G1", "G2", "G6",
    "F3", "F7", "M3", "M7", "N0", "E5", "H1", "H2", "H6", "G3", "F5", "J1", "G7", "M5", "U6", "V0", "H3",
    "U4", "U5", "U3", "H7", "J2", "U1", "J3", "U0", "N1", "J4", "J6", "V2", "J7", "V1", "G5", "V3", "v3",
    "u5", "u6", "Q1", "H5", "u1", "u0", "v0", "v1", "J5", "u4", "v2", "u3", "U2", "u2", "X", "Q0",
]


def nn(a, b):
    return lax.dot_general(a, b, (((1,), (0,)), ((), ())), preferred_element_type=F32)


def nt(a, b):
    return lax.dot_general(a, b, (((1,), (1,)), ((), ())), preferred_element_type=F32)


def tn(a, b):
    return lax.dot_general(a, b, (((0,), (0,)), ((), ())), preferred_element_type=F32)


def names():
    found = [f"z{a}" for a in "abcdef"] + [f"y{a}" for a in "abcdefgh"]
    for u in range(8):
        found += [f"{n}{u}" for n in (
            "r1", "r2p", "r2m", "r3ep", "r3em", "r3lp", "r3lm", "gp", "gm", "g2p", "g2m", "g3", "h3")]
        found += [f"hd{u}"] if u in DIRECT else [f"{n}{u}" for n in ("gd", "hp", "hm", "h2p", "h2m")]
        if u > 1:
            found += [f"opp{u}", f"opm{u}"]
    for r in range(2):
        found += [f"{n}{r}" for n in ("d2p", "d2m", "dep", "dem", "dlp", "dlm", "dz")]
    return found


NAMES = names()
INDEX = {name: i for i, name in enumerate(NAMES)}


def kernel(tok_h, win_h, wout_h, gain_h, cot_h,
           out_h, gtok_h, gwin_h, gwout_h,
           win, wout, gain, TC, PP, RB, X2, X1, SG, OP, YB2, YB1, ZS, ZB, OS, WI, WO,
           ssem, rsem, lsem):
    row, col, d = lax.axis_index("row"), lax.axis_index("col"), lax.axis_index("dp")
    zh, y = row // 4, row % 4
    x, c = col // 2, col % 2
    z = 2 * zh + d
    sib, e = 1 - c, 1 - d

    def dev(xx=None, cc=None, yy=None, zz=None):
        xx = x if xx is None else xx
        cc = c if cc is None else cc
        yy = y if yy is None else yy
        zz = z if zz is None else zz
        return (4 * (zz // 2) + yy, 2 * xx + cc, zz % 2)

    xp, xm, xo = (x + 1) % 4, (x + 3) % 4, (x + 2) % 4
    yp, ym = (y + 1) % 4, (y + 3) % 4
    zp, zm, zo = (z + 1) % 4, (z + 3) % 4, (z + 2) % 4
    to_xp, to_xm = dev(xx=xp), dev(xx=xm)
    to_yp, to_ym = dev(yy=yp), dev(yy=ym)
    to_zp, to_zm, to_zo = dev(zz=zp), dev(zz=zm), dev(zz=zo)
    to_sib = dev(cc=sib)
    to_dp = (row, col, e)

    sent = {}
    arrived = set()

    def send(name, src, dst, to):
        i = INDEX[name]
        copy = pltpu.make_async_remote_copy(
            src_ref=src, dst_ref=dst, send_sem=ssem.at[i], recv_sem=rsem.at[i],
            device_id=to, device_id_type=pl.DeviceIdType.MESH)
        copy.start()
        sent[name] = copy

    def same(name, ref, to):
        send(name, ref, ref, to)

    def got(*wanted):
        for name in wanted:
            if name not in arrived:
                arrived.add(name)
                sent[name].wait_recv()

    loads = [
        pltpu.make_async_copy(tok_h, TC.at[d, 0, y, zh], lsem.at[0]),
        pltpu.make_async_copy(cot_h, TC.at[d, 1, y, zh], lsem.at[1]),
        pltpu.make_async_copy(win_h, win, lsem.at[2]),
        pltpu.make_async_copy(wout_h, wout, lsem.at[3]),
        pltpu.make_async_copy(gain_h, gain, lsem.at[4]),
    ]
    stores = []

    def store(src, dst, i):
        copy = pltpu.make_async_copy(src, dst, lsem.at[i])
        copy.start()
        stores.append(copy)

    def at(u):
        return (y + u // 2) % 4, (zh + u % 2) % 2

    def both(dd, u):
        yy, hh = at(u)
        return TC.at[dd, :, yy, hh]

    def one(dd, kind, u):
        yy, hh = at(u)
        return TC.at[dd, kind, yy, hh]

    def zslot(zz, kind):
        return TC.at[zz % 2, kind, y, zz // 2]

    def start():
        for load in loads:
            load.start()
        barrier = pltpu.get_barrier_semaphore()
        for to in (to_xp, to_xm, to_yp, to_ym, to_zp, to_zm, to_zo, to_sib):
            pl.semaphore_signal(barrier, inc=1, device_id=to, device_id_type=pl.DeviceIdType.MESH)
        pl.semaphore_wait(barrier, 8)
        loads[0].wait()
        loads[1].wait()
        same("za", zslot(z, 0), to_zp)
        same("zb", zslot(z, 1), to_zm)
        same("ya", both(d, 0), to_yp)
        same("yb", both(d, 0), to_ym)

    def weights():
        for load in loads[2:]:
            load.wait()

    def along_z(n):
        if n == 1:
            got("za")
            same("ze", zslot(zm, 0), to_zp)
        elif n == 2:
            got("zb")
            same("zf", zslot(zp, 1), to_zm)
        else:
            same("zc", zslot(z, 1), to_zp)
            same("zd", zslot(z, 0), to_zm)

    def along_y(n):
        if n == 1:
            got("ze", "zf")
            same("yc", both(d, 1), to_yp)
            same("yd", both(d, 1), to_ym)
            return
        name, sends, kind, u, to = {
            2: ("ya", "ye", 0, 6, to_yp),
            3: ("yb", "yf", 1, 2, to_ym),
            4: ("yc", "yg", 0, 7, to_yp),
            5: ("yd", "yh", 1, 3, to_ym),
        }[n]
        got(name)
        same(sends, one(d, kind, u), to)

    SOURCES = {0: (), 1: ("ze", "zf"), 6: ("ya",), 2: ("yb",), 4: ("ye", "yf"),
               7: ("yc",), 3: ("yd",), 5: ("yg", "yh")}

    def inputs_across(u):
        got(*SOURCES[u])
        same(f"opp{u}", one(d, 0, u), to_zp)
        same(f"opm{u}", one(d, 1, u), to_zm)

    def first_products(u):
        got(*SOURCES[u])
        yy, hh = at(u)

        def tile(n, carry):
            cols = pl.ds(pl.multiple_of(n * TILE, TILE), TILE)
            shape = (2, 4, SUB, TILE)
            PP[u, 0, :, :, :, cols] = nn(TC[d, 0, yy, hh], win[:, cols]).astype(BF).reshape(shape)
            PP[u, 1, :, :, :, cols] = nt(TC[d, 1, yy, hh], wout[cols, :]).astype(BF).reshape(shape)
            return carry

        lax.fori_loop(0, HID // TILE, tile, 0)
        send(f"r1{u}", PP.at[u, :, sib], RB.at[u], to_sib)

    def pair(u, kind, q):
        return PP[u, kind, c, q].astype(F32) + RB[u, kind, q].astype(F32)

    def reduce_far(u):
        got(f"r1{u}")
        for name, kind, q, to, dst in (
            ("r2p", 0, xo, to_xp, X2.at[u, 0]),
            ("r2m", 1, xo, to_xm, X2.at[u, 1]),
            ("r3ep", 1, xp, to_xp, X1.at[u, 0, 1]),
            ("r3em", 0, xm, to_xm, X1.at[u, 1, 0]),
        ):
            PP[u, kind, c, q] = pair(u, kind, q).astype(BF)
            send(f"{name}{u}", PP.at[u, kind, c, q], dst, to)

    def reduce_near(u):
        for name, sends, kind, q, to in (
            ("r2p", "r3lp", 0, xp, to_xp),
            ("r2m", "r3lm", 1, xm, to_xm),
        ):
            got(f"{name}{u}")
            PP[u, kind, c, q] = (pair(u, kind, q) + X2[u, kind].astype(F32)).astype(BF)
            send(f"{sends}{u}", PP.at[u, kind, c, q], X1.at[u, kind, kind], to)

    def activate(u):
        got(f"r3ep{u}", f"r3em{u}", f"r3lp{u}", f"r3lm{u}")
        yy, hh = at(u)
        sums = [
            pair(u, kind, x) + X1[u, 0, kind].astype(F32) + X1[u, 1, kind].astype(F32)
            for kind in range(2)
        ]
        g = gain[...]
        scaled = sums[0] * g
        total = jnp.zeros_like(scaled)
        slope = jnp.zeros_like(scaled)
        for level in range(LEVELS):
            sig = jax.nn.sigmoid(SHARP * (scaled - (level + 0.5)))
            total = total + sig
            slope = slope + sig * (1.0 - sig)
        SG[d, 0, yy, hh, c, x] = total.astype(BF)
        SG[d, 1, yy, hh, c, x] = (sums[1] * (slope * (SHARP * g))).astype(BF)
        block = SG.at[d, :, yy, hh, c, x]
        same(f"gp{u}", block, to_xp)
        same(f"gm{u}", block, to_xm)
        if u not in DIRECT:
            same(f"gd{u}", block, to_dp)

    def forward(u, g, dd):
        yy, hh = at(u)
        got(f"{g}p{u}")
        same(f"{g}2p{u}", SG.at[dd, 0, yy, hh, c, xm], to_xp)
        got(f"{g}m{u}")
        same(f"{g}2m{u}", SG.at[dd, 1, yy, hh, c, xp], to_xm)

    def half_done(u):
        got(f"g2p{u}", f"g2m{u}")
        yy, hh = at(u)
        rows = SG.at[d, :, yy, hh, c]
        same(f"g3{u}", rows, to_sib)
        if u in DIRECT:
            same(f"hd{u}", rows, to_dp)

    def share_other(u):
        got(f"gd{u}")
        yy, hh = at(u)
        block = SG.at[e, :, yy, hh, c, x]
        same(f"hp{u}", block, to_xp)
        same(f"hm{u}", block, to_xm)

    def other_half_done(u):
        if u in DIRECT:
            got(f"hd{u}")
        else:
            got(f"h2p{u}", f"h2m{u}")
        yy, hh = at(u)
        same(f"h3{u}", SG.at[e, :, yy, hh, c], to_sib)

    def second_products(u):
        got(f"g3{u}")
        k, r = u // 2, u % 2
        yy, hh = at(u)

        def tile(n, carry):
            cols = pl.ds(pl.multiple_of(n * TILE, TILE), TILE)
            a = SG[d, 0, yy, hh].reshape(BLK, HID)
            OP[k, r, 0, :, cols] = nn(a, wout[:, cols]).astype(BF)
            b = SG[d, 1, yy, hh].reshape(BLK, HID)
            OP[k, r, 1, :, cols] = nt(b, win[cols, :]).astype(BF)
            return carry

        lax.fori_loop(0, FEAT // TILE, tile, 0)
        if k == 2:
            send(f"d2p{r}", OP.at[2, r, 0], YB2.at[r, 0], to_yp)
            send(f"d2m{r}", OP.at[2, r, 1], YB2.at[r, 1], to_ym)
        elif k == 1:
            send(f"dep{r}", OP.at[1, r, 1], YB1.at[r, 0, 1], to_yp)
        elif k == 3:
            send(f"dem{r}", OP.at[3, r, 0], YB1.at[r, 1, 0], to_ym)

    def strips(fn):
        def strip(i, carry):
            fn(pl.ds(pl.multiple_of(i * 32, 32), 32))
            return carry
        lax.fori_loop(0, BLK // 32, strip, 0)

    def out_late(r):
        for name, sends, k, kind, to in (
            ("d2p", "dlp", 1, 0, to_yp),
            ("d2m", "dlm", 3, 1, to_ym),
        ):
            got(f"{name}{r}")

            def add(rows):
                OP[k, r, kind, rows] = (
                    OP[k, r, kind, rows].astype(F32) + YB2[r, kind, rows].astype(F32)
                ).astype(BF)

            strips(add)
            send(f"{sends}{r}", OP.at[k, r, kind], YB1.at[r, kind, kind], to)

    def out_sum(kind, r, rows):
        return (OP[0, r, kind, rows].astype(F32) + YB1[r, 0, kind, rows].astype(F32)
                + YB1[r, 1, kind, rows].astype(F32))

    def finish(r):
        for kind in range(2):
            got(f"{('dlp', 'dep')[kind]}{r}", f"{('dem', 'dlm')[kind]}{r}")
            if r == 1:
                def add(rows):
                    ZS[kind, rows] = out_sum(kind, 1, rows).astype(BF)

                strips(add)
                send(f"dz{kind}", ZS.at[kind], ZB.at[kind], to_zo)
            else:
                got(f"dz{kind}")

                def add(rows):
                    OS[kind, rows] = (out_sum(kind, 0, rows) + ZB[kind, rows].astype(F32)).astype(BF)

                strips(add)
                store(OS.at[kind], (out_h, gtok_h)[kind], 5 + kind)

    def own_ready():
        got(*[f"g3{u}" for u in range(8)], *[s for u in range(8) for s in SOURCES[u]])

    def other_ready(units):
        got("za", "zb", "zc", "zd", *[f"h3{u}" for u in units])
        got(*[f"op{a}{u}" for u in units if u > 1 for a in "pm"])

    def out_left(dd, cols):
        return SG[dd, 0, :, :, :, :, :, cols].reshape(8 * BLK, TILE)

    def grad_out_own(n):
        own_ready()
        cols = slice(n * TILE, (n + 1) * TILE)
        WO[cols, :] = tn(out_left(d, cols), TC[d, 1].reshape(8 * BLK, FEAT)).astype(BF)

    def grad_in_own(n):
        own_ready()
        cols = slice(n * TILE, (n + 1) * TILE)
        left = TC[d, 0, :, :, :, cols].reshape(8 * BLK, TILE)
        WI[cols, :] = tn(left, SG[d, 1].reshape(8 * BLK, HID)).astype(BF)

    def grad_out_add(cols, ks):
        value = WO[cols, :].astype(F32)
        for k in ks:
            yy = (y + k) % 4
            left = SG[e, 0, yy, :, :, :, :, cols].reshape(2 * BLK, TILE)
            value = value + tn(left, TC[e, 1, yy].reshape(2 * BLK, FEAT))
        WO[cols, :] = value.astype(BF)

    def grad_in_add(cols, ks):
        value = WI[cols, :].astype(F32)
        for k in ks:
            yy = (y + k) % 4
            left = TC[e, 0, yy, :, :, cols].reshape(2 * BLK, TILE)
            value = value + tn(left, SG[e, 1, yy].reshape(2 * BLK, HID))
        WI[cols, :] = value.astype(BF)

    def grad_other(n, add):
        other_ready((0, 1, 2, 3, 6, 7))
        add(slice(n * TILE, (n + 1) * TILE), (0, 1, 3))

    def grad_last():
        other_ready(range(8))
        for add, rows, buffer, place, i in (
            (grad_out_add, HID, WO, gwout_h, 7),
            (grad_in_add, FEAT, WI, gwin_h, 8),
        ):
            def tile(n, carry):
                add(pl.ds(pl.multiple_of(n * TILE, TILE), TILE), (2,))
                return carry

            lax.fori_loop(0, rows // TILE, tile, 0)
            store(buffer, place, i)

    steps = {
        "I": start, "L": weights, "Z": along_z, "Y": along_y, "P": inputs_across,
        "A": first_products, "B": reduce_far, "C": reduce_near, "D": activate,
        "E": lambda u: forward(u, "g", d), "F": half_done,
        "G": share_other, "H": lambda u: forward(u, "h", e), "J": other_half_done,
        "M": second_products, "N": out_late, "Q": finish,
        "U": grad_out_own, "V": grad_in_own,
        "u": lambda n: grad_other(n, grad_out_add),
        "v": lambda n: grad_other(n, grad_in_add),
        "X": grad_last,
    }
    for step in ORDER:
        steps[step[0]](*[int(a) for a in step[1:]])
    for copy in stores:
        copy.wait()
    for name in NAMES:
        sent[name].wait_send()


def shards(tokens, w_in, w_out, spike_gain, cotangent):
    anywhere = pl.BlockSpec(memory_space=pl.ANY)
    vmem = pltpu.VMEM
    n = len(NAMES)
    return pl.pallas_call(
        kernel,
        out_shape=(
            jax.ShapeDtypeStruct((BLK, FEAT), BF),
            jax.ShapeDtypeStruct((BLK, FEAT), BF),
            jax.ShapeDtypeStruct((FEAT, HID), BF),
            jax.ShapeDtypeStruct((HID, FEAT), BF),
        ),
        in_specs=[anywhere] * 5,
        out_specs=[anywhere] * 4,
        scratch_shapes=[
            vmem((FEAT, HID), BF),
            vmem((HID, FEAT), BF),
            vmem((1, HID), F32),
            vmem((2, 2, 4, 2, BLK, FEAT), BF),
            vmem((8, 2, 2, 4, SUB, HID), BF),
            vmem((8, 2, 4, SUB, HID), BF),
            vmem((8, 2, SUB, HID), BF),
            vmem((8, 2, 2, SUB, HID), BF),
            vmem((2, 2, 4, 2, 2, 4, SUB, HID), BF),
            vmem((4, 2, 2, BLK, FEAT), BF),
            vmem((2, 2, BLK, FEAT), BF),
            vmem((2, 2, 2, BLK, FEAT), BF),
            vmem((2, BLK, FEAT), BF),
            vmem((2, BLK, FEAT), BF),
            vmem((2, BLK, FEAT), BF),
            vmem((FEAT, HID), BF),
            vmem((HID, FEAT), BF),
            pltpu.SemaphoreType.DMA((n,)),
            pltpu.SemaphoreType.DMA((n,)),
            pltpu.SemaphoreType.DMA((9,)),
        ],
        compiler_params=pltpu.CompilerParams(
            collective_id=0, has_side_effects=True, vmem_limit_bytes=64 << 20
        ),
        name="spiking_block",
    )(tokens, w_in, w_out, spike_gain.reshape(1, HID), cotangent)


def solution(mesh):
    placed = (
        P(("dp", "row"), "col"),
        P("col", "row"),
        P("row", "col"),
        P("row"),
        P(("dp", "row"), "col"),
    )
    return jax.shard_map(
        shards,
        mesh=mesh,
        in_specs=placed,
        out_specs=(
            P(("dp", "row"), "col"),
            P(("dp", "row"), "col"),
            P("col", "row"),
            P("row", "col"),
        ),
        check_vma=False,
    )
```

```python
import jax
import jax.numpy as jnp
from jax import lax
from jax.experimental import pallas as pl
from jax.experimental.pallas import tpu as pltpu
from jax.sharding import PartitionSpec as P

LEVELS = 4
SHARP = 4.0
BF = jnp.bfloat16
F32 = jnp.float32
FEAT, HID, BLK = 1024, 1792, 128
SUB = 16
TILE = 256
WIDE = 896

DIRECT = (0, 1)

ORDER = [
    "I", "L", "A0", "B0", "C0", "Z2", "Z1", "D0", "A2", "P6", "A6", "B2", "Y1", "B6", "A1", "E0", "Z3", "Y3",
    "C6", "B1", "C2", "F0", "Y2", "C1", "P2", "D6", "D2", "P3", "Y4", "Y5", "D1", "A7", "A3", "B7", "A4",
    "E6", "E2", "E1", "C7", "B3", "A5", "F6", "F2", "F1", "B5", "B4", "M0", "C3", "M1", "C5", "C4", "M6",
    "D7", "M2", "D5", "D3", "E5", "P7", "D4", "E7", "E3", "F5", "E4", "P4", "P5", "G6", "F7", "M5", "G2",
    "F3", "M7", "G3", "F4", "M3", "G7", "U3", "H6", "U2", "V2", "U1", "J0", "N1", "H2", "H3", "V3", "U5",
    "H7", "G4", "U0", "G5", "V0", "J2", "U6", "J1", "J3", "J6", "M4", "J7", "U4", "V1", "Q1", "H4", "u4",
    "u6", "H5", "u1", "u0", "v3", "v2", "N0", "J5", "J4", "v0", "u2", "u3", "u5", "v1", "X", "Q0",
]


def nn(a, b):
    return lax.dot_general(a, b, (((1,), (0,)), ((), ())), preferred_element_type=F32)


def nt(a, b):
    return lax.dot_general(a, b, (((1,), (1,)), ((), ())), preferred_element_type=F32)


def tn(a, b):
    return lax.dot_general(a, b, (((0,), (0,)), ((), ())), preferred_element_type=F32)


def names():
    found = [f"z{a}" for a in "abcdef"] + [f"y{a}" for a in "abcdefgh"]
    for u in range(8):
        found += [f"{n}{u}" for n in (
            "r1", "r2p", "r2m", "r3ep", "r3em", "r3lp", "r3lm", "gp", "gm", "g2p", "g2m", "g3", "h3")]
        found += [f"hd{u}"] if u in DIRECT else [f"{n}{u}" for n in ("gd", "hp", "hm", "h2p", "h2m")]
        if u > 1:
            found += [f"opp{u}", f"opm{u}"]
    for r in range(2):
        found += [f"{n}{r}" for n in ("d2p", "d2m", "dep", "dem", "dlp", "dlm", "dz")]
    return found


NAMES = names()
INDEX = {name: i for i, name in enumerate(NAMES)}


def kernel(tok_h, win_h, wout_h, gain_h, cot_h,
           out_h, gtok_h, gwin_h, gwout_h,
           win, wout, gain, TC, PP, RB, X2, X1, SG, OP, YB2, YB1, ZS, ZB, OS, WI, WO,
           ssem, rsem, lsem):
    row, col, d = lax.axis_index("row"), lax.axis_index("col"), lax.axis_index("dp")
    zh, y = row // 4, row % 4
    x, c = col // 2, col % 2
    z = 2 * zh + d
    sib, e = 1 - c, 1 - d

    def dev(xx=None, cc=None, yy=None, zz=None):
        xx = x if xx is None else xx
        cc = c if cc is None else cc
        yy = y if yy is None else yy
        zz = z if zz is None else zz
        return (4 * (zz // 2) + yy, 2 * xx + cc, zz % 2)

    xp, xm, xo = (x + 1) % 4, (x + 3) % 4, (x + 2) % 4
    yp, ym = (y + 1) % 4, (y + 3) % 4
    zp, zm, zo = (z + 1) % 4, (z + 3) % 4, (z + 2) % 4
    to_xp, to_xm = dev(xx=xp), dev(xx=xm)
    to_yp, to_ym = dev(yy=yp), dev(yy=ym)
    to_zp, to_zm, to_zo = dev(zz=zp), dev(zz=zm), dev(zz=zo)
    to_sib = dev(cc=sib)
    to_dp = (row, col, e)

    sent = {}
    arrived = set()

    def send(name, src, dst, to):
        i = INDEX[name]
        copy = pltpu.make_async_remote_copy(
            src_ref=src, dst_ref=dst, send_sem=ssem.at[i], recv_sem=rsem.at[i],
            device_id=to, device_id_type=pl.DeviceIdType.MESH)
        copy.start()
        sent[name] = copy

    def same(name, ref, to):
        send(name, ref, ref, to)

    def got(*wanted):
        for name in wanted:
            if name not in arrived:
                arrived.add(name)
                sent[name].wait_recv()

    loads = [
        pltpu.make_async_copy(tok_h, TC.at[d, 0, y, zh], lsem.at[0]),
        pltpu.make_async_copy(cot_h, TC.at[d, 1, y, zh], lsem.at[1]),
        pltpu.make_async_copy(win_h, win, lsem.at[2]),
        pltpu.make_async_copy(wout_h, wout, lsem.at[3]),
        pltpu.make_async_copy(gain_h, gain, lsem.at[4]),
    ]
    stores = []

    def store(src, dst, i):
        copy = pltpu.make_async_copy(src, dst, lsem.at[i])
        copy.start()
        stores.append(copy)

    def at(u):
        return (y + u // 2) % 4, (zh + u % 2) % 2

    def both(dd, u):
        yy, hh = at(u)
        return TC.at[dd, :, yy, hh]

    def one(dd, kind, u):
        yy, hh = at(u)
        return TC.at[dd, kind, yy, hh]

    def zslot(zz, kind):
        return TC.at[zz % 2, kind, y, zz // 2]

    def start():
        for load in loads:
            load.start()
        barrier = pltpu.get_barrier_semaphore()
        for to in (to_xp, to_xm, to_yp, to_ym, to_zp, to_zm, to_zo, to_sib):
            pl.semaphore_signal(barrier, inc=1, device_id=to, device_id_type=pl.DeviceIdType.MESH)
        pl.semaphore_wait(barrier, 8)
        loads[0].wait()
        loads[1].wait()
        same("za", zslot(z, 0), to_zp)
        same("zb", zslot(z, 1), to_zm)
        same("ya", both(d, 0), to_yp)
        same("yb", both(d, 0), to_ym)

    def weights():
        for load in loads[2:]:
            load.wait()

    def along_z(n):
        if n == 1:
            got("za")
            same("ze", zslot(zm, 0), to_zp)
        elif n == 2:
            got("zb")
            same("zf", zslot(zp, 1), to_zm)
        else:
            same("zc", zslot(z, 1), to_zp)
            same("zd", zslot(z, 0), to_zm)

    def along_y(n):
        if n == 1:
            got("ze", "zf")
            same("yc", both(d, 1), to_yp)
            same("yd", both(d, 1), to_ym)
            return
        name, sends, kind, u, to = {
            2: ("ya", "ye", 0, 6, to_yp),
            3: ("yb", "yf", 1, 2, to_ym),
            4: ("yc", "yg", 0, 7, to_yp),
            5: ("yd", "yh", 1, 3, to_ym),
        }[n]
        got(name)
        same(sends, one(d, kind, u), to)

    SOURCES = {0: (), 1: ("ze", "zf"), 6: ("ya",), 2: ("yb",), 4: ("ye", "yf"),
               7: ("yc",), 3: ("yd",), 5: ("yg", "yh")}

    def inputs_across(u):
        got(*SOURCES[u])
        same(f"opp{u}", one(d, 0, u), to_zp)
        same(f"opm{u}", one(d, 1, u), to_zm)

    def first_products(u):
        got(*SOURCES[u])
        yy, hh = at(u)

        def tile(n, carry):
            cols = pl.ds(pl.multiple_of(n * WIDE, WIDE), WIDE)
            shape = (2, 4, SUB, WIDE)
            PP[u, 0, :, :, :, cols] = nn(TC[d, 0, yy, hh], win[:, cols]).astype(BF).reshape(shape)
            PP[u, 1, :, :, :, cols] = nt(TC[d, 1, yy, hh], wout[cols, :]).astype(BF).reshape(shape)
            return carry

        lax.fori_loop(0, HID // WIDE, tile, 0)
        send(f"r1{u}", PP.at[u, :, sib], RB.at[u], to_sib)

    def pair(u, kind, q):
        return PP[u, kind, c, q].astype(F32) + RB[u, kind, q].astype(F32)

    def reduce_far(u):
        got(f"r1{u}")
        for name, kind, q, to, dst in (
            ("r2p", 0, xo, to_xp, X2.at[u, 0]),
            ("r2m", 1, xo, to_xm, X2.at[u, 1]),
            ("r3ep", 1, xp, to_xp, X1.at[u, 0, 1]),
            ("r3em", 0, xm, to_xm, X1.at[u, 1, 0]),
        ):
            PP[u, kind, c, q] = pair(u, kind, q).astype(BF)
            send(f"{name}{u}", PP.at[u, kind, c, q], dst, to)

    def reduce_near(u):
        for name, sends, kind, q, to in (
            ("r2p", "r3lp", 0, xp, to_xp),
            ("r2m", "r3lm", 1, xm, to_xm),
        ):
            got(f"{name}{u}")
            PP[u, kind, c, q] = (pair(u, kind, q) + X2[u, kind].astype(F32)).astype(BF)
            send(f"{sends}{u}", PP.at[u, kind, c, q], X1.at[u, kind, kind], to)

    def activate(u):
        got(f"r3ep{u}", f"r3em{u}", f"r3lp{u}", f"r3lm{u}")
        yy, hh = at(u)
        sums = [
            pair(u, kind, x) + X1[u, 0, kind].astype(F32) + X1[u, 1, kind].astype(F32)
            for kind in range(2)
        ]
        g = gain[...].reshape(1, HID)
        scaled = sums[0] * g
        total = jnp.zeros_like(scaled)
        slope = jnp.zeros_like(scaled)
        for level in range(LEVELS):
            sig = jax.nn.sigmoid(SHARP * (scaled - (level + 0.5)))
            total = total + sig
            slope = slope + sig * (1.0 - sig)
        SG[d, 0, yy, hh, c, x] = total.astype(BF)
        SG[d, 1, yy, hh, c, x] = (sums[1] * (slope * (SHARP * g))).astype(BF)
        block = SG.at[d, :, yy, hh, c, x]
        same(f"gp{u}", block, to_xp)
        same(f"gm{u}", block, to_xm)
        if u not in DIRECT:
            same(f"gd{u}", block, to_dp)

    def forward(u, g, dd):
        yy, hh = at(u)
        got(f"{g}p{u}")
        same(f"{g}2p{u}", SG.at[dd, 0, yy, hh, c, xm], to_xp)
        got(f"{g}m{u}")
        same(f"{g}2m{u}", SG.at[dd, 1, yy, hh, c, xp], to_xm)

    def half_done(u):
        got(f"g2p{u}", f"g2m{u}")
        yy, hh = at(u)
        rows = SG.at[d, :, yy, hh, c]
        same(f"g3{u}", rows, to_sib)
        if u in DIRECT:
            same(f"hd{u}", rows, to_dp)

    def share_other(u):
        got(f"gd{u}")
        yy, hh = at(u)
        block = SG.at[e, :, yy, hh, c, x]
        same(f"hp{u}", block, to_xp)
        same(f"hm{u}", block, to_xm)

    def other_half_done(u):
        if u in DIRECT:
            got(f"hd{u}")
        else:
            got(f"h2p{u}", f"h2m{u}")
        yy, hh = at(u)
        same(f"h3{u}", SG.at[e, :, yy, hh, c], to_sib)

    def second_products(u):
        got(f"g3{u}")
        k, r = u // 2, u % 2
        yy, hh = at(u)

        a = SG[d, 0, yy, hh].reshape(BLK, HID)
        OP[k, r, 0] = nn(a, wout[...]).astype(BF)
        b = SG[d, 1, yy, hh].reshape(BLK, HID)
        OP[k, r, 1] = nt(b, win[...]).astype(BF)
        if k == 2:
            send(f"d2p{r}", OP.at[2, r, 0], YB2.at[r, 0], to_yp)
            send(f"d2m{r}", OP.at[2, r, 1], YB2.at[r, 1], to_ym)
        elif k == 1:
            send(f"dep{r}", OP.at[1, r, 1], YB1.at[r, 0, 1], to_yp)
        elif k == 3:
            send(f"dem{r}", OP.at[3, r, 0], YB1.at[r, 1, 0], to_ym)

    def strips(fn):
        def strip(i, carry):
            fn(pl.ds(pl.multiple_of(i * 32, 32), 32))
            return carry
        lax.fori_loop(0, BLK // 32, strip, 0)

    def out_late(r):
        for name, sends, k, kind, to in (
            ("d2p", "dlp", 1, 0, to_yp),
            ("d2m", "dlm", 3, 1, to_ym),
        ):
            got(f"{name}{r}")

            def add(rows):
                OP[k, r, kind, rows] = (
                    OP[k, r, kind, rows].astype(F32) + YB2[r, kind, rows].astype(F32)
                ).astype(BF)

            strips(add)
            send(f"{sends}{r}", OP.at[k, r, kind], YB1.at[r, kind, kind], to)

    def out_sum(kind, r, rows):
        return (OP[0, r, kind, rows].astype(F32) + YB1[r, 0, kind, rows].astype(F32)
                + YB1[r, 1, kind, rows].astype(F32))

    def finish(r):
        for kind in range(2):
            got(f"{('dlp', 'dep')[kind]}{r}", f"{('dem', 'dlm')[kind]}{r}")
            if r == 1:
                def add(rows):
                    ZS[kind, rows] = out_sum(kind, 1, rows).astype(BF)

                strips(add)
                send(f"dz{kind}", ZS.at[kind], ZB.at[kind], to_zo)
            else:
                got(f"dz{kind}")

                def add(rows):
                    OS[kind, rows] = (out_sum(kind, 0, rows) + ZB[kind, rows].astype(F32)).astype(BF)

                strips(add)
                store(OS.at[kind], (out_h, gtok_h)[kind], 5 + kind)

    def own_ready():
        got(*[f"g3{u}" for u in range(8)], *[s for u in range(8) for s in SOURCES[u]])

    def other_ready(units):
        got("za", "zb", "zc", "zd", *[f"h3{u}" for u in units])
        got(*[f"op{a}{u}" for u in units if u > 1 for a in "pm"])

    def out_left(dd, cols):
        return SG[dd, 0, :, :, :, :, :, cols].reshape(8 * BLK, TILE)

    def grad_out_own(n):
        own_ready()
        cols = slice(n * TILE, (n + 1) * TILE)
        WO[cols, :] = tn(out_left(d, cols), TC[d, 1].reshape(8 * BLK, FEAT)).astype(BF)

    def grad_in_own(n):
        own_ready()
        cols = slice(n * TILE, (n + 1) * TILE)
        left = TC[d, 0, :, :, :, cols].reshape(8 * BLK, TILE)
        WI[cols, :] = tn(left, SG[d, 1].reshape(8 * BLK, HID)).astype(BF)

    def grad_out_add(cols, ks):
        value = WO[cols, :].astype(F32)
        for k in ks:
            yy = (y + k) % 4
            left = SG[e, 0, yy, :, :, :, :, cols].reshape(2 * BLK, TILE)
            value = value + tn(left, TC[e, 1, yy].reshape(2 * BLK, FEAT))
        WO[cols, :] = value.astype(BF)

    def grad_in_add(cols, ks):
        value = WI[cols, :].astype(F32)
        for k in ks:
            yy = (y + k) % 4
            left = TC[e, 0, yy, :, :, cols].reshape(2 * BLK, TILE)
            value = value + tn(left, SG[e, 1, yy].reshape(2 * BLK, HID))
        WI[cols, :] = value.astype(BF)

    def grad_other(n, add):
        other_ready((0, 1, 2, 3, 6, 7))
        add(slice(n * TILE, (n + 1) * TILE), (0, 1, 3))

    def grad_last():
        other_ready(range(8))
        for add, rows, buffer, place, i in (
            (grad_out_add, HID, WO, gwout_h, 7),
            (grad_in_add, FEAT, WI, gwin_h, 8),
        ):
            def tile(n, carry):
                add(pl.ds(pl.multiple_of(n * TILE, TILE), TILE), (2,))
                return carry

            lax.fori_loop(0, rows // TILE, tile, 0)
            store(buffer, place, i)

    steps = {
        "I": start, "L": weights, "Z": along_z, "Y": along_y, "P": inputs_across,
        "A": first_products, "B": reduce_far, "C": reduce_near, "D": activate,
        "E": lambda u: forward(u, "g", d), "F": half_done,
        "G": share_other, "H": lambda u: forward(u, "h", e), "J": other_half_done,
        "M": second_products, "N": out_late, "Q": finish,
        "U": grad_out_own, "V": grad_in_own,
        "u": lambda n: grad_other(n, grad_out_add),
        "v": lambda n: grad_other(n, grad_in_add),
        "X": grad_last,
    }
    for step in ORDER:
        steps[step[0]](*[int(a) for a in step[1:]])
    for copy in stores:
        copy.wait()
    for name in NAMES:
        sent[name].wait_send()


PARTS = ((1, 128), (1, 128), (8, 128), (8, 224))


def hand_over_kernel(*refs):
    ins, outs, bufs, sems = refs[:4], refs[4:8], refs[8:12], refs[12]
    copies = []
    i = 0
    for a, b, o, (n, rows) in zip(ins, bufs, outs, PARTS):
        for j in range(n):
            part = pl.ds(j * rows, rows)
            copies.append((
                pltpu.make_async_copy(a.at[part], b.at[part], sems.at[i]),
                pltpu.make_async_copy(b.at[part], o.at[part], sems.at[i + 1]),
            ))
            i += 2
    for load, _ in copies:
        load.start()
    for load, keep in copies:
        load.wait()
        keep.start()
    for _, keep in copies:
        keep.wait()


def hand_over(results):
    anywhere = pl.BlockSpec(memory_space=pl.ANY)
    return pl.pallas_call(
        hand_over_kernel,
        out_shape=tuple(jax.ShapeDtypeStruct(r.shape, r.dtype) for r in results),
        in_specs=[anywhere] * 4,
        out_specs=[anywhere] * 4,
        scratch_shapes=[pltpu.VMEM(r.shape, r.dtype) for r in results]
        + [pltpu.SemaphoreType.DMA((2 * sum(n for n, _ in PARTS),))],
        compiler_params=pltpu.CompilerParams(vmem_limit_bytes=63 << 20),
        name="hand_over",
    )(*results)


def shards(tokens, w_in, w_out, spike_gain, cotangent):
    anywhere = pl.BlockSpec(memory_space=pl.ANY)
    vmem = pltpu.VMEM
    n = len(NAMES)
    results = pl.pallas_call(
        kernel,
        out_shape=(
            jax.ShapeDtypeStruct((BLK, FEAT), BF),
            jax.ShapeDtypeStruct((BLK, FEAT), BF),
            jax.ShapeDtypeStruct((FEAT, HID), BF),
            jax.ShapeDtypeStruct((HID, FEAT), BF),
        ),
        in_specs=[anywhere] * 5,
        out_specs=[anywhere] * 4,
        scratch_shapes=[
            vmem((FEAT, HID), BF),
            vmem((HID, FEAT), BF),
            vmem((HID,), F32),
            vmem((2, 2, 4, 2, BLK, FEAT), BF),
            vmem((8, 2, 2, 4, SUB, HID), BF),
            vmem((8, 2, 4, SUB, HID), BF),
            vmem((8, 2, SUB, HID), BF),
            vmem((8, 2, 2, SUB, HID), BF),
            vmem((2, 2, 4, 2, 2, 4, SUB, HID), BF),
            vmem((4, 2, 2, BLK, FEAT), BF),
            vmem((2, 2, BLK, FEAT), BF),
            vmem((2, 2, 2, BLK, FEAT), BF),
            vmem((2, BLK, FEAT), BF),
            vmem((2, BLK, FEAT), BF),
            vmem((2, BLK, FEAT), BF),
            vmem((FEAT, HID), BF),
            vmem((HID, FEAT), BF),
            pltpu.SemaphoreType.DMA((n,)),
            pltpu.SemaphoreType.DMA((n,)),
            pltpu.SemaphoreType.DMA((9,)),
        ],
        compiler_params=pltpu.CompilerParams(
            collective_id=0, has_side_effects=True, vmem_limit_bytes=64 << 20
        ),
        name="spiking_block",
    )(tokens, w_in, w_out, spike_gain, cotangent)
    return hand_over(results)


def solution(mesh):
    placed = (
        P(("dp", "row"), "col"),
        P("col", "row"),
        P("row", "col"),
        P("row"),
        P(("dp", "row"), "col"),
    )
    return jax.shard_map(
        shards,
        mesh=mesh,
        in_specs=placed,
        out_specs=(
            P(("dp", "row"), "col"),
            P(("dp", "row"), "col"),
            P("col", "row"),
            P("row", "col"),
        ),
        check_vma=False,
    )
```

```python
import jax
import jax.numpy as jnp
from jax import lax
from jax.experimental import pallas as pl
from jax.experimental.pallas import tpu as pltpu
from jax.sharding import PartitionSpec as P

LEVELS = 4
SHARP = 4.0
BF = jnp.bfloat16
F32 = jnp.float32
FEAT, HID, BLK = 1024, 1792, 128
SUB = 16
TILE = 256
WIDE = 896

DIRECT = (0, 6, 2)
AROUND = (2, 3, 4, 5)

ORDER = [
    "I", "L", "T0", "A0", "B0", "Z2", "Z1", "C0", "A2", "D0", "A6", "Y1", "B2", "Y3", "Y2", "Z3", "B6", "P2",
    "E0", "A1", "C2", "T1", "C6", "B1", "F0", "D2", "D6", "C1", "Y5", "A3", "Y4", "A7", "E2", "E6", "B7",
    "P4", "A4", "B3", "F6", "M0", "B4", "P5", "A5", "F2", "C3", "B5", "M6", "C4", "C5", "C7", "P3", "D3",
    "D5", "D7", "E5", "E3", "M2", "D1", "F5", "J2", "E7", "D4", "J0", "F3", "P6", "P7", "M5", "E1", "F7",
    "M3", "E4", "G7", "M7", "F1", "G1", "G3", "N10", "F4", "G5", "J6", "M1", "N11", "M4", "U2", "U4", "U3",
    "H1", "H7", "U0", "H3", "V2", "G4", "Q10", "U6", "U1", "J1", "V1", "J7", "U5", "Q11", "J3", "H5", "V0",
    "N00", "u4", "u0", "v1", "u3", "N01", "H4", "v2", "V3", "J5", "v3", "t3", "v0", "u1", "Q00", "J4", "s1",
    "Q01", "u2", "u5", "s5", "s0", "u6", "s6", "X", "s2", "t2", "s3", "s4", "t0", "t1",
]


def nn(a, b):
    return lax.dot_general(a, b, (((1,), (0,)), ((), ())), preferred_element_type=F32)


def tn(a, b):
    return lax.dot_general(a, b, (((0,), (0,)), ((), ())), preferred_element_type=F32)


def names():
    found = [f"z{a}" for a in "abcdef"] + [f"y{a}" for a in "abcdefgh"]
    for u in range(8):
        found += [f"{n}{u}" for n in (
            "r1", "r2p", "r2m", "r3ep", "r3em", "r3lp", "r3lm", "gp", "gm", "g2p", "g2m", "g3", "h3")]
        found += [f"hd{u}"] if u in DIRECT else [f"{n}{u}" for n in ("gd", "hp", "hm", "h2p", "h2m")]
        if u > 1:
            found += [f"opp{u}", f"opm{u}"]
    for r in range(2):
        found += [f"dep{r}", f"dem{r}"]
        found += [f"{n}{r}{h}" for n in ("d2p", "d2m", "dlp", "dlm", "dz") for h in range(2)]
    return found


NAMES = names()
INDEX = {name: i for i, name in enumerate(NAMES)}


def kernel(tok_h, win_h, wout_h, gain_h, cot_h,
           out_h, gtok_h, gwin_h, gwout_h, lastsg_h, lasttc_h,
           win, wout, gain, TC, PP, RB, X2, X1, SG, OP, YB2, YB1, ZS, ZB, OS, WI, WO,
           ssem, rsem, lsem):
    row, col, d = lax.axis_index("row"), lax.axis_index("col"), lax.axis_index("dp")
    zh, y = row // 4, row % 4
    x, c = col // 2, col % 2
    z = 2 * zh + d
    sib, e = 1 - c, 1 - d

    def dev(xx=None, cc=None, yy=None, zz=None):
        xx = x if xx is None else xx
        cc = c if cc is None else cc
        yy = y if yy is None else yy
        zz = z if zz is None else zz
        return (4 * (zz // 2) + yy, 2 * xx + cc, zz % 2)

    xp, xm, xo = (x + 1) % 4, (x + 3) % 4, (x + 2) % 4
    yp, ym = (y + 1) % 4, (y + 3) % 4
    zp, zm, zo = (z + 1) % 4, (z + 3) % 4, (z + 2) % 4
    to_xp, to_xm = dev(xx=xp), dev(xx=xm)
    to_yp, to_ym = dev(yy=yp), dev(yy=ym)
    to_zp, to_zm, to_zo = dev(zz=zp), dev(zz=zm), dev(zz=zo)
    to_sib = dev(cc=sib)
    to_dp = (row, col, e)
    to_nd = dev(zz=(z + 2 * d + 3) % 4)

    sent = {}
    arrived = set()

    def send(name, src, dst, to):
        i = INDEX[name]
        copy = pltpu.make_async_remote_copy(
            src_ref=src, dst_ref=dst, send_sem=ssem.at[i], recv_sem=rsem.at[i],
            device_id=to, device_id_type=pl.DeviceIdType.MESH)
        copy.start()
        sent[name] = copy

    def same(name, ref, to):
        send(name, ref, ref, to)

    def got(*wanted):
        for name in wanted:
            if name not in arrived:
                arrived.add(name)
                sent[name].wait_recv()

    loads = [
        pltpu.make_async_copy(tok_h, TC.at[d, 0, y, zh], lsem.at[0]),
        pltpu.make_async_copy(cot_h, TC.at[d, 1, y, zh], lsem.at[1]),
        pltpu.make_async_copy(win_h, win, lsem.at[2]),
        pltpu.make_async_copy(wout_h, wout, lsem.at[3]),
        pltpu.make_async_copy(gain_h, gain, lsem.at[4]),
    ]
    stores = []

    def store(src, dst, i):
        copy = pltpu.make_async_copy(src, dst, lsem.at[i])
        copy.start()
        stores.append(copy)

    def at(u):
        return (y + u // 2) % 4, (zh + u % 2) % 2

    def both(dd, u):
        yy, hh = at(u)
        return TC.at[dd, :, yy, hh]

    def one(dd, kind, u):
        yy, hh = at(u)
        return TC.at[dd, kind, yy, hh]

    def zslot(zz, kind):
        return TC.at[zz % 2, kind, y, zz // 2]

    def start():
        for load in loads:
            load.start()
        barrier = pltpu.get_barrier_semaphore()
        for to in (to_xp, to_xm, to_yp, to_ym, to_zp, to_zm, to_zo, to_sib):
            pl.semaphore_signal(barrier, inc=1, device_id=to, device_id_type=pl.DeviceIdType.MESH)
        pl.semaphore_wait(barrier, 8)
        loads[0].wait()
        loads[1].wait()
        same("za", zslot(z, 0), to_zp)
        same("zb", zslot(z, 1), to_zm)
        same("ya", both(d, 0), to_yp)
        same("yb", both(d, 0), to_ym)

    def weights():
        for load in loads[2:]:
            load.wait()

    def flip(n):
        source, place, rows = ((wout, WI, HID), (win, WO, FEAT))[n]
        for i in range(rows // TILE):
            part = slice(i * TILE, (i + 1) * TILE)
            place[:, part] = source[part, :].T

    def along_z(n):
        if n == 1:
            got("za")
            same("ze", zslot(zm, 0), to_zp)
        elif n == 2:
            got("zb")
            same("zf", zslot(zp, 1), to_zm)
        else:
            same("zc", zslot(z, 1), to_zp)
            same("zd", zslot(z, 0), to_zm)

    def along_y(n):
        if n == 1:
            got("ze", "zf")
            same("yc", both(d, 1), to_yp)
            same("yd", both(d, 1), to_ym)
            return
        name, sends, kind, u, to = {
            2: ("ya", "ye", 0, 6, to_yp),
            3: ("yb", "yf", 1, 2, to_ym),
            4: ("yc", "yg", 0, 7, to_yp),
            5: ("yd", "yh", 1, 3, to_ym),
        }[n]
        got(name)
        same(sends, one(d, kind, u), to)

    SOURCES = {0: (), 1: ("ze", "zf"), 6: ("ya",), 2: ("yb",), 4: ("ye", "yf"),
               7: ("yc",), 3: ("yd",), 5: ("yg", "yh")}

    def inputs_across(u):
        got(*SOURCES[u])
        same(f"opp{u}", one(d, 0, u), to_nd if u in AROUND else to_zp)
        same(f"opm{u}", one(d, 1, u), to_nd if u in AROUND else to_zm)

    def first_products(u):
        got(*SOURCES[u])
        yy, hh = at(u)

        def tile(n, carry):
            cols = pl.ds(pl.multiple_of(n * WIDE, WIDE), WIDE)
            shape = (2, 4, SUB, WIDE)
            PP[u, 0, :, :, :, cols] = nn(TC[d, 0, yy, hh], win[:, cols]).astype(BF).reshape(shape)
            PP[u, 1, :, :, :, cols] = nn(TC[d, 1, yy, hh], WI[:, cols]).astype(BF).reshape(shape)
            return carry

        lax.fori_loop(0, HID // WIDE, tile, 0)
        send(f"r1{u}", PP.at[u, :, sib], RB.at[u], to_sib)

    def pair(u, kind, q):
        return PP[u, kind, c, q].astype(F32) + RB[u, kind, q].astype(F32)

    def reduce_far(u):
        got(f"r1{u}")
        for name, kind, q, to, dst in (
            ("r2p", 0, xo, to_xp, X2.at[u, 0]),
            ("r2m", 1, xo, to_xm, X2.at[u, 1]),
            ("r3ep", 1, xp, to_xp, X1.at[u, 0, 1]),
            ("r3em", 0, xm, to_xm, X1.at[u, 1, 0]),
        ):
            PP[u, kind, c, q] = pair(u, kind, q).astype(BF)
            send(f"{name}{u}", PP.at[u, kind, c, q], dst, to)

    def reduce_near(u):
        for name, sends, kind, q, to in (
            ("r2p", "r3lp", 0, xp, to_xp),
            ("r2m", "r3lm", 1, xm, to_xm),
        ):
            got(f"{name}{u}")
            PP[u, kind, c, q] = (pair(u, kind, q) + X2[u, kind].astype(F32)).astype(BF)
            send(f"{sends}{u}", PP.at[u, kind, c, q], X1.at[u, kind, kind], to)

    def activate(u):
        got(f"r3ep{u}", f"r3em{u}", f"r3lp{u}", f"r3lm{u}")
        yy, hh = at(u)
        sums = [
            pair(u, kind, x) + X1[u, 0, kind].astype(F32) + X1[u, 1, kind].astype(F32)
            for kind in range(2)
        ]
        g = gain[...].reshape(1, HID)
        scaled = sums[0] * g
        total = jnp.zeros_like(scaled)
        slope = jnp.zeros_like(scaled)
        for level in range(LEVELS):
            sig = jax.nn.sigmoid(SHARP * (scaled - (level + 0.5)))
            total = total + sig
            slope = slope + sig * (1.0 - sig)
        SG[d, 0, yy, hh, c, x] = total.astype(BF)
        SG[d, 1, yy, hh, c, x] = (sums[1] * (slope * (SHARP * g))).astype(BF)
        block = SG.at[d, :, yy, hh, c, x]
        same(f"gp{u}", block, to_xp)
        same(f"gm{u}", block, to_xm)
        if u not in DIRECT:
            same(f"gd{u}", block, to_dp)

    def forward(u, g, dd):
        yy, hh = at(u)
        got(f"{g}p{u}")
        same(f"{g}2p{u}", SG.at[dd, 0, yy, hh, c, xm], to_xp)
        got(f"{g}m{u}")
        same(f"{g}2m{u}", SG.at[dd, 1, yy, hh, c, xp], to_xm)

    def half_done(u):
        got(f"g2p{u}", f"g2m{u}")
        yy, hh = at(u)
        rows = SG.at[d, :, yy, hh, c]
        same(f"g3{u}", rows, to_sib)
        if u in DIRECT:
            same(f"hd{u}", rows, to_dp)

    def share_other(u):
        got(f"gd{u}")
        yy, hh = at(u)
        block = SG.at[e, :, yy, hh, c, x]
        same(f"hp{u}", block, to_xp)
        same(f"hm{u}", block, to_xm)

    def other_half_done(u):
        if u in DIRECT:
            got(f"hd{u}")
        else:
            got(f"h2p{u}", f"h2m{u}")
        yy, hh = at(u)
        same(f"h3{u}", SG.at[e, :, yy, hh, c], to_sib)

    def second_products(u):
        got(f"g3{u}")
        k, r = u // 2, u % 2
        yy, hh = at(u)

        a = SG[d, 0, yy, hh].reshape(BLK, HID)
        OP[k, r, 0] = nn(a, wout[...]).astype(BF)
        b = SG[d, 1, yy, hh].reshape(BLK, HID)
        OP[k, r, 1] = nn(b, WO[...]).astype(BF)
        if k == 2:
            for h in range(2):
                rows = pl.ds(h * 64, 64)
                send(f"d2p{r}{h}", OP.at[2, r, 0, rows], YB2.at[r, 0, rows], to_yp)
                send(f"d2m{r}{h}", OP.at[2, r, 1, rows], YB2.at[r, 1, rows], to_ym)
        elif k == 1:
            send(f"dep{r}", OP.at[1, r, 1], YB1.at[r, 0, 1], to_yp)
        elif k == 3:
            send(f"dem{r}", OP.at[3, r, 0], YB1.at[r, 1, 0], to_ym)

    def strips(h, fn):
        for i in range(2):
            fn(pl.ds(h * 64 + i * 32, 32))

    def out_late(r, h):
        part = pl.ds(h * 64, 64)
        for name, sends, k, kind, to in (
            ("d2p", "dlp", 1, 0, to_yp),
            ("d2m", "dlm", 3, 1, to_ym),
        ):
            got(f"{name}{r}{h}")

            def add(rows):
                OP[k, r, kind, rows] = (
                    OP[k, r, kind, rows].astype(F32) + YB2[r, kind, rows].astype(F32)
                ).astype(BF)

            strips(h, add)
            send(f"{sends}{r}{h}", OP.at[k, r, kind, part], YB1.at[r, kind, kind, part], to)

    def out_sum(kind, r, rows):
        return (OP[0, r, kind, rows].astype(F32) + YB1[r, 0, kind, rows].astype(F32)
                + YB1[r, 1, kind, rows].astype(F32))

    def finish(r, h):
        part = pl.ds(h * 64, 64)
        for kind in range(2):
            got(*((f"dlp{r}{h}", f"dem{r}") if kind == 0 else (f"dep{r}", f"dlm{r}{h}")))
            if r == 1:
                def add(rows):
                    ZS[kind, rows] = out_sum(kind, 1, rows).astype(BF)

                strips(h, add)
                send(f"dz{kind}{h}", ZS.at[kind, part], ZB.at[kind, part], to_zo)
            else:
                got(f"dz{kind}{h}")

                def add(rows):
                    OS[kind, rows] = (out_sum(kind, 0, rows) + ZB[kind, rows].astype(F32)).astype(BF)

                strips(h, add)
                store(OS.at[kind, part], (out_h, gtok_h)[kind].at[part], 5 + 2 * kind + h)

    def own_ready():
        got(*[f"g3{u}" for u in range(8)], *[s for u in range(8) for s in SOURCES[u]])

    def other_ready(units):
        got("za", "zb", "zc", "zd", *[f"h3{u}" for u in units])
        got(*[f"op{a}{u}" for u in units if u > 1 for a in "pm"])

    def out_left(dd, cols):
        return SG[dd, 0, :, :, :, :, :, cols].reshape(8 * BLK, TILE)

    def grad_out_own(n):
        own_ready()
        cols = slice(n * TILE, (n + 1) * TILE)
        WO[cols, :] = tn(out_left(d, cols), TC[d, 1].reshape(8 * BLK, FEAT)).astype(BF)

    def grad_in_own(n):
        own_ready()
        cols = slice(n * TILE, (n + 1) * TILE)
        left = TC[d, 0, :, :, :, cols].reshape(8 * BLK, TILE)
        WI[cols, :] = tn(left, SG[d, 1].reshape(8 * BLK, HID)).astype(BF)

    def grad_out_add(cols, ks):
        value = WO[cols, :].astype(F32)
        for k in ks:
            yy = (y + k) % 4
            left = SG[e, 0, yy, :, :, :, :, cols].reshape(2 * BLK, TILE)
            value = value + tn(left, TC[e, 1, yy].reshape(2 * BLK, FEAT))
        WO[cols, :] = value.astype(BF)

    def grad_in_add(cols, ks):
        value = WI[cols, :].astype(F32)
        for k in ks:
            yy = (y + k) % 4
            left = TC[e, 0, yy, :, :, cols].reshape(2 * BLK, TILE)
            value = value + tn(left, SG[e, 1, yy].reshape(2 * BLK, HID))
        WI[cols, :] = value.astype(BF)

    def grad_other(n, add):
        other_ready((0, 1, 6, 7))
        add(slice(n * TILE, (n + 1) * TILE), (0, 3))

    def grad_rest(n, add, buffer, place, i):
        other_ready((2, 3))
        rows = slice(n * TILE, (n + 1) * TILE)
        add(rows, (1,))
        store(buffer.at[rows], place.at[rows], i + n)

    def keep_last():
        other_ready((4, 5))
        for hh in range(2):
            for c2 in range(2):
                for q in range(4):
                    row = hh * BLK + c2 * 64 + q * SUB
                    for kind in range(2):
                        store(SG.at[e, kind, (y + 2) % 4, hh, c2, q],
                              lastsg_h.at[kind, pl.ds(row, SUB)], 20 + kind * 16 + row // SUB)
            for kind in range(2):
                store(TC.at[e, kind, (y + 2) % 4, hh],
                      lasttc_h.at[kind, pl.ds(hh * BLK, BLK)], 52 + 2 * kind + hh)

    steps = {
        "I": start, "L": weights, "T": flip, "Z": along_z, "Y": along_y, "P": inputs_across,
        "A": first_products, "B": reduce_far, "C": reduce_near, "D": activate,
        "E": lambda u: forward(u, "g", d), "F": half_done,
        "G": share_other, "H": lambda u: forward(u, "h", e), "J": other_half_done,
        "M": second_products, "N": out_late, "Q": finish,
        "U": grad_out_own, "V": grad_in_own,
        "u": lambda n: grad_other(n, grad_out_add),
        "v": lambda n: grad_other(n, grad_in_add),
        "s": lambda n: grad_rest(n, grad_out_add, WO, gwout_h, 9),
        "t": lambda n: grad_rest(n, grad_in_add, WI, gwin_h, 16),
        "X": keep_last,
    }
    for step in ORDER:
        steps[step[0]](*[int(a) for a in step[1:]])
    for copy in stores:
        copy.wait()
    for name in NAMES:
        sent[name].wait_send()


def hand_over_kernel(a_out, a_tok, a_in, a_wout, a_sg, a_tc, o_out, o_tok, o_in, o_wout,
                     b_out, b_tok, b_in, b_wout, sg, tc, lsem, ssem):
    arrive = [(a_sg, sg), (a_tc, tc)]
    leave = []
    for source, buffer, place, n in (
        (a_wout, b_wout, o_wout, HID // TILE),
        (a_in, b_in, o_in, FEAT // TILE),
    ):
        for j in range(n):
            rows = pl.ds(j * TILE, TILE)
            arrive.append((source.at[rows], buffer.at[rows]))
            leave.append((buffer.at[rows], place.at[rows]))
    arrive += [(a_out, b_out), (a_tok, b_tok)]
    leave += [(b_out, o_out), (b_tok, o_tok)]
    loads = [pltpu.make_async_copy(a, b, lsem.at[i]) for i, (a, b) in enumerate(arrive)]
    keeps = [pltpu.make_async_copy(a, b, ssem.at[i]) for i, (a, b) in enumerate(leave)]
    for load in loads:
        load.start()
    loads[0].wait()
    loads[1].wait()
    for i, keep in enumerate(keeps):
        loads[i + 2].wait()
        if i < HID // TILE:
            rows = slice(i * TILE, (i + 1) * TILE)
            b_wout[rows, :] = (b_wout[rows, :].astype(F32) + tn(sg[0, :, rows], tc[1])).astype(BF)
        elif i < HID // TILE + FEAT // TILE:
            j = i - HID // TILE
            rows = slice(j * TILE, (j + 1) * TILE)
            b_in[rows, :] = (b_in[rows, :].astype(F32) + tn(tc[0, :, rows], sg[1])).astype(BF)
        keep.start()
    for keep in keeps:
        keep.wait()


def hand_over(results):
    anywhere = pl.BlockSpec(memory_space=pl.ANY)
    return pl.pallas_call(
        hand_over_kernel,
        out_shape=tuple(jax.ShapeDtypeStruct(r.shape, r.dtype) for r in results[:4]),
        in_specs=[anywhere] * 6,
        out_specs=[anywhere] * 4,
        scratch_shapes=[pltpu.VMEM(r.shape, r.dtype) for r in results]
        + [pltpu.SemaphoreType.DMA((15,)), pltpu.SemaphoreType.DMA((13,))],
        compiler_params=pltpu.CompilerParams(vmem_limit_bytes=63 << 20),
        name="hand_over",
    )(*results)


def shards(tokens, w_in, w_out, spike_gain, cotangent):
    anywhere = pl.BlockSpec(memory_space=pl.ANY)
    vmem = pltpu.VMEM
    n = len(NAMES)
    results = pl.pallas_call(
        kernel,
        out_shape=(
            jax.ShapeDtypeStruct((BLK, FEAT), BF),
            jax.ShapeDtypeStruct((BLK, FEAT), BF),
            jax.ShapeDtypeStruct((FEAT, HID), BF),
            jax.ShapeDtypeStruct((HID, FEAT), BF),
            jax.ShapeDtypeStruct((2, 2 * BLK, HID), BF),
            jax.ShapeDtypeStruct((2, 2 * BLK, FEAT), BF),
        ),
        in_specs=[anywhere] * 5,
        out_specs=[anywhere] * 6,
        scratch_shapes=[
            vmem((FEAT, HID), BF),
            vmem((HID, FEAT), BF),
            vmem((HID,), F32),
            vmem((2, 2, 4, 2, BLK, FEAT), BF),
            vmem((8, 2, 2, 4, SUB, HID), BF),
            vmem((8, 2, 4, SUB, HID), BF),
            vmem((8, 2, SUB, HID), BF),
            vmem((8, 2, 2, SUB, HID), BF),
            vmem((2, 2, 4, 2, 2, 4, SUB, HID), BF),
            vmem((4, 2, 2, BLK, FEAT), BF),
            vmem((2, 2, BLK, FEAT), BF),
            vmem((2, 2, 2, BLK, FEAT), BF),
            vmem((2, BLK, FEAT), BF),
            vmem((2, BLK, FEAT), BF),
            vmem((2, BLK, FEAT), BF),
            vmem((FEAT, HID), BF),
            vmem((HID, FEAT), BF),
            pltpu.SemaphoreType.DMA((n,)),
            pltpu.SemaphoreType.DMA((n,)),
            pltpu.SemaphoreType.DMA((56,)),
        ],
        compiler_params=pltpu.CompilerParams(
            collective_id=0, has_side_effects=True, vmem_limit_bytes=64 << 20
        ),
        name="spiking_block",
    )(tokens, w_in, w_out, spike_gain, cotangent)
    return hand_over(results)


def solution(mesh):
    placed = (
        P(("dp", "row"), "col"),
        P("col", "row"),
        P("row", "col"),
        P("row"),
        P(("dp", "row"), "col"),
    )
    return jax.shard_map(
        shards,
        mesh=mesh,
        in_specs=placed,
        out_specs=(
            P(("dp", "row"), "col"),
            P(("dp", "row"), "col"),
            P("col", "row"),
            P("row", "col"),
        ),
        check_vma=False,
    )
```
